32 devices in a mesh: fsdp: 4 (over x, core), ctx: 4 (over z), tp: 2 (over y).
Axes of the slice: x: 2, y: 2, z: 4, core: 2. Of those that a mesh axis runs over, the one named last changes fastest.
Arguments:
- inputs: bfloat16 [1024, 4, 2048], P('ctx', 'fsdp'), may hold values from -6 to 6
- segments: int32 [4, 1024], P('fsdp', 'ctx'), may hold values from 0 to 3, never falling along the last dimension, each value on 1 to 512 neighbouring positions
- norm_attn: bfloat16 [2048], P('fsdp'), may hold values from 0.5 to 1.5
- query_weight: bfloat16 [2048, 2048], P('fsdp', 'tp'), may hold values from -0.4375 to 0.4375
- key_weight: bfloat16 [2048, 512], P('fsdp', 'tp'), may hold values from -0.4375 to 0.4375
- value_weight: bfloat16 [2048, 512], P('fsdp', 'tp'), may hold values from -0.125 to 0.125
- out_weight: bfloat16 [2048, 2048], P('tp', 'fsdp'), may hold values from -3 to 3
- norm_mlp: bfloat16 [2048], P('fsdp'), may hold values from 0.5 to 1.5
- gate_weight: bfloat16 [2048, 8192], P('fsdp', 'tp'), may hold values from -0.125 to 0.125
- up_weight: bfloat16 [2048, 8192], P('fsdp', 'tp'), may hold values from -0.125 to 0.125
- down_weight: bfloat16 [8192, 2048], P('tp', 'fsdp'), may hold values from -0.5 to 0.5
- thresholds: float32 [32], P('tp'), may hold values from 0.1 to 0.5
- cotangent: bfloat16 [1024, 4, 2048], P('ctx', 'fsdp'), may hold values from -6 to 6
Outputs:
- output: bfloat16 [1024, 4, 2048], P('ctx', 'fsdp')
- input_grad: float32 [1024, 4, 2048], P('ctx', 'fsdp')
- grad_norm_attn: float32 [2048], P('fsdp')
- grad_query: float32 [2048, 2048], P('fsdp', 'tp')
- grad_key: float32 [2048, 512], P('fsdp', 'tp')
- grad_value: float32 [2048, 512], P('fsdp', 'tp')
- grad_out: float32 [2048, 2048], P('tp', 'fsdp')
- grad_norm_mlp: float32 [2048], P('fsdp')
- grad_gate: float32 [2048, 8192], P('fsdp', 'tp')
- grad_up: float32 [2048, 8192], P('fsdp', 'tp')
- grad_down: float32 [8192, 2048], P('tp', 'fsdp')
- head_peaks: float32 [32], P('tp')
- clipped_query: bfloat16 [2048, 2048], P('fsdp', 'tp')
- clipped_key: bfloat16 [2048, 512], P('fsdp', 'tp')
The draws below stay inside these ranges and needn't reach their ends.
Inputs may be any that keep to these rules, and one draw needn't show every extreme that they name: `segments`: within each sequence the document number never falls; every document spans 1 to 512 positions, and one spans exactly 512.
All inputs are finite; a program needn't handle non-finite values.
Results may differ from the reference program's by a relative error of at most 0.022.
Values may be sent and summed in bfloat16 or wider, within the bound.
No kernel may reach another device: no remote copies, remote signals or barrier semaphores. Data moves between devices by JAX's collectives and lax.ppermute only.
A program may use at most 320 MiB of HBM per device.

```python
import math
import jax
import jax.numpy as jnp
import numpy as np
from jax import lax

D = 2048
NH = 32
KVH = 8
HD = 64
FF = 8192
BLOCK = 256
LENGTH = 1024
SEQS_ALL = 4


def block_levels(stream_key, dims, cuts, smallest, top_value):
    level, own = 1.0, jax.random.fold_in(stream_key, 6)
    for position, parts in cuts:
        heights = jnp.exp(jax.random.uniform(jax.random.fold_in(own, position), (parts,), jnp.float32, smallest / len(cuts), top_value / len(cuts)))
        level = level * jnp.repeat(heights, dims[position] // parts).reshape([-1 if axis == position else 1 for axis in range(len(dims))])
    return level


def profile(number_of, total, bound, slope):
    portions = [(1 << 20) // math.isqrt(standing ** slope) + 1 for standing in range(2, number_of + 1)]
    spare, given = total - bound - (number_of - 1), [1] * (number_of - 1)
    while spare > 0:
        movable = [i for i in range(number_of - 1) if given[i] < bound]
        mass, left = sum([portions[i] for i in movable]), spare
        for i in movable:
            addition = min(bound - given[i], max(1, left * portions[i] // mass), spare)
            given[i] = given[i] + addition
            spare = spare - addition
    return np.array([bound] + given)


def uneven_parts(key, count, total, most, slope):
    if count == 2:
        one = jax.random.randint(key, (), max(1, total - most), min(most, total - 1) + 1)
        return jnp.stack([one, total - one])
    lengths = jnp.asarray(profile(count, total, most, slope), jnp.int32)
    pairs = (count - 1) // 2
    giver, sink = lengths[1:1 + 2 * pairs:2], lengths[2:2 + 2 * pairs:2]
    margin = jnp.minimum(giver - 1, most - sink)
    moved = jax.random.randint(jax.random.fold_in(key, 1), (pairs,), 0, 1 << 20) % (margin + 1)
    lengths = lengths.at[1:1 + 2 * pairs:2].set(giver - moved).at[2:2 + 2 * pairs:2].set(sink + moved)
    return lengths[jax.random.permutation(jax.random.fold_in(key, 2), count)]


def bell_draw(own_key, extent, width, limit, cuts=(), kind=jnp.bfloat16):
    drawn = jax.random.normal(own_key, extent, jnp.float32) * width
    if len(cuts) > 0:
        drawn = block_levels(own_key, extent, cuts, -0.22, 0.18) * drawn
    return jnp.clip(drawn, min=-limit, max=limit).astype(kind)


def setup_inputs(seed: int = 0) -> dict:
    key_of = jax.random.split(jax.random.key(seed), 14)
    return {
        "inputs": bell_draw(key_of[0], (LENGTH, SEQS_ALL, D), 1.0, 6.0, ((0, 4), (1, 4))),
        "segments": jax.vmap(lambda own: jnp.searchsorted(jnp.cumsum(uneven_parts(own, 4, LENGTH, LENGTH // 2, 1)), jnp.arange(LENGTH), side="right"))(jax.random.split(key_of[1], SEQS_ALL)).reshape((SEQS_ALL, LENGTH)).astype(jnp.int32),
        "norm_attn": jnp.clip(1.0 + 0.1 * jax.random.normal(key_of[2], (D,), jnp.float32), 0.5, 1.5).astype(jnp.bfloat16),
        "query_weight": bell_draw(key_of[3], (D, NH * HD), (D // 12) ** -0.5, 0.4375, ((0, 4), (1, 2))),
        "key_weight": bell_draw(key_of[4], (D, KVH * HD), (D // 12) ** -0.5, 0.4375, ((0, 4), (1, 2))),
        "value_weight": bell_draw(key_of[5], (D, KVH * HD), D ** -0.5, 0.125, ((0, 4), (1, 2))),
        "out_weight": bell_draw(key_of[6], (NH * HD, D), 4 ** -0.5, 3.0, ((0, 2), (1, 4))),
        "norm_mlp": jnp.clip(1.0 + 0.1 * jax.random.normal(key_of[7], (D,), jnp.float32), 0.5, 1.5).astype(jnp.bfloat16),
        "gate_weight": bell_draw(key_of[8], (D, FF), D ** -0.5, 0.125, ((0, 4), (1, 2))),
        "up_weight": bell_draw(key_of[9], (D, FF), D ** -0.5, 0.125, ((0, 4), (1, 2))),
        "down_weight": bell_draw(key_of[10], (FF, D), (FF // 64) ** -0.5, 0.5, ((0, 2), (1, 4))),
        "thresholds": jnp.clip(jnp.exp(math.log(0.5) - 1.609438 * jax.random.uniform(key_of[11], (NH,), jnp.float32) ** block_levels(key_of[11], (NH,), ((0, 2),), -0.2, 0.2)), 0.1, 0.5),
        "cotangent": bell_draw(key_of[12], (LENGTH, SEQS_ALL, D), 1.0, 6.0, ((0, 4), (1, 4))),
    }


NORM_EPSILON = 1e-05
ROPE_BASE = 10000000.0
RESIDUAL = 0.22
ATTN_SCALE = 1.0 / 64.0

@jax.custom_vjp
def low(v):
    return lax.optimization_barrier(v.astype(jnp.bfloat16)).astype(jnp.float32)

@jax.custom_vjp
def low_back(v):
    return v

def low_keep(v):
    return (low(v), None)

def low_pass(kept, grad):
    return (grad,)

def back_keep(v):
    return (v, None)

def back_low(kept, grad):
    return (low(grad),)
low.defvjp(low_keep, low_pass)
low_back.defvjp(back_keep, back_low)

def highest_dot(left_mat, right_mat):
    return jnp.dot(left_mat, right_mat, precision=lax.Precision.HIGHEST)

def rope_angles(positions, head_size):
    half_size = head_size // 2
    freqs = ROPE_BASE ** (-(jnp.arange(half_size, dtype=jnp.float32) * 2.0 / head_size))
    angle = positions.astype(jnp.float32)[:, None] * freqs[None, :]
    return (jnp.cos(angle), jnp.sin(angle))

def rotate(values, cosine, sine_table):
    half_size = values.shape[-1] // 2
    front_half = values[..., :half_size]
    back_half = values[..., half_size:]
    cos_wide = cosine[:, None, :]
    sin_wide = sine_table[:, None, :]
    return jnp.concatenate([front_half * cos_wide - back_half * sin_wide, back_half * cos_wide + front_half * sin_wide], axis=-1)

def rms_normed(values):
    return values * lax.rsqrt(lax.optimization_barrier(jnp.mean(values * values, axis=-1, keepdims=True)) + NORM_EPSILON)

def block_layer(inputs, seg_row, gain_attn, query_w, key_w, value_w, out_w, gain_mlp, gate_w, up_w, down_w):
    length = inputs.shape[0]
    hidden_one = low(rms_normed(inputs) * gain_attn)
    query_lin = low_back(highest_dot(hidden_one, query_w))
    key_lin = low_back(highest_dot(hidden_one, key_w))
    value_vec = low_back(low(highest_dot(hidden_one, value_w)))
    positions = jnp.arange(length, dtype=jnp.int32)
    cosine, sine_table = rope_angles(positions, HD)
    queries = low(rotate(query_lin.reshape(length, NH, HD), cosine, sine_table))
    key_heads = low(rotate(key_lin.reshape(length, KVH, HD), cosine, sine_table))
    value_heads = value_vec.reshape(length, KVH, HD)
    grouped = queries.reshape(length, KVH, NH // KVH, HD)
    key_blk = positions // BLOCK
    row_size = math.gcd(length, 512)
    row_blocks = length // row_size

    def attend(block_data):
        block_q, block_pos, block_seg = block_data
        scores = low_back(jnp.einsum('qhgd,khd->hgqk', block_q, key_heads, precision=lax.Precision.HIGHEST) * ATTN_SCALE)
        allowed = (block_seg[:, None] == seg_row[None, :]) & ((block_pos // BLOCK)[:, None] >= key_blk[None, :])
        masked = jnp.where(allowed[None, None], scores, -jnp.inf)
        row_peak = lax.optimization_barrier(jnp.max(masked, axis=-1, keepdims=True))
        exp_total = lax.optimization_barrier(jnp.sum(jnp.exp(masked - row_peak), axis=-1, keepdims=True))
        weights_low = low(jnp.exp(masked - row_peak - jnp.log(exp_total)))
        mixture = jnp.einsum('hgqk,khd->qhgd', weights_low, value_heads, precision=lax.Precision.HIGHEST)
        return (mixture, lax.optimization_barrier(jnp.max(masked, axis=(2, 3))))
    mixture, head_peaks = lax.map(jax.checkpoint(attend), (grouped.reshape(row_blocks, row_size, KVH, NH // KVH, HD), positions.reshape(row_blocks, row_size), seg_row.reshape(row_blocks, row_size)))
    attn_out = low_back(low(mixture.reshape(length, NH * HD)))
    attn_sum = low_back(highest_dot(attn_out, out_w))
    middle = inputs + RESIDUAL * attn_sum
    hidden_two = low(rms_normed(middle) * gain_mlp)
    gate_val = low_back(highest_dot(hidden_two, gate_w))
    up_val = low_back(highest_dot(hidden_two, up_w))
    inner_act = low(jax.nn.silu(gate_val) * up_val)
    mlp_sum = low_back(highest_dot(inner_act, down_w))
    return (middle + RESIDUAL * mlp_sum, lax.optimization_barrier(jnp.max(head_peaks, axis=0)).reshape(NH))

def reference(inputs, segments, norm_attn, query_weight, key_weight, value_weight, out_weight, norm_mlp, gate_weight, up_weight, down_weight, thresholds, cotangent):
    params = tuple((matrix.astype(jnp.float32) for matrix in (norm_attn, query_weight, key_weight, value_weight, out_weight, norm_mlp, gate_weight, up_weight, down_weight)))
    seq_inputs = jnp.swapaxes(inputs.astype(jnp.float32), 0, 1)
    seq_cotan = jnp.swapaxes(cotangent.astype(jnp.float32), 0, 1)

    def per_sequence(state_now, block_data):
        grad_sums, best_peak = state_now
        seq_in, seq_row, seq_cot = block_data

        def forward(seq_x, *weights):
            return block_layer(seq_x, seq_row, *weights)
        result, backward, seq_peaks = jax.vjp(forward, seq_in, *params, has_aux=True)
        gradients = backward(seq_cot)
        grad_sums = tuple((summed + update for summed, update in zip(grad_sums, gradients[1:])))
        return ((grad_sums, jnp.maximum(best_peak, seq_peaks)), (result.astype(jnp.bfloat16), gradients[0]))
    start_state = (tuple((jnp.zeros_like(matrix) for matrix in params)), jnp.full((NH,), -jnp.inf, jnp.float32))
    (grad_sums, best_peak), (outputs, grad_inputs) = lax.scan(per_sequence, start_state, (seq_inputs, segments, seq_cotan))
    ratio_clip = thresholds / jnp.maximum(best_peak, thresholds)
    query_factor = jnp.repeat(jnp.sqrt(ratio_clip), HD)
    key_factor = jnp.repeat(jnp.sqrt(lax.optimization_barrier(jnp.min(ratio_clip.reshape(KVH, NH // KVH), axis=1))), HD)
    clipped_query = (params[1] * query_factor[None, :]).astype(jnp.bfloat16)
    clipped_key = (params[2] * key_factor[None, :]).astype(jnp.bfloat16)
    return (jnp.swapaxes(outputs, 0, 1), jnp.swapaxes(grad_inputs, 0, 1), grad_sums[0], grad_sums[1], grad_sums[2], grad_sums[3], grad_sums[4], grad_sums[5], grad_sums[6], grad_sums[7], grad_sums[8], best_peak, clipped_query, clipped_key)
```

```python
import jax
import jax.numpy as jnp
from jax import lax
from jax.sharding import PartitionSpec as P

HD = 64
BLOCK = 256

NORM_EPSILON = 1e-05
ROPE_BASE = 10000000.0
RESIDUAL = 0.22
ATTN_SCALE = 1.0 / 64.0
NEG_FILL = -1e30


F32 = jnp.float32
BF16 = jnp.bfloat16


def matmul_plain(left_mat, right_mat):
    return jnp.dot(left_mat, right_mat, preferred_element_type=F32)


def contract_rows(left_mat, right_mat):
    return lax.dot_general(
        left_mat, right_mat, (((0,), (0,)), ((), ())), preferred_element_type=F32
    )


def contract_cols(left_mat, right_mat):
    return lax.dot_general(
        left_mat, right_mat, (((1,), (1,)), ((), ())), preferred_element_type=F32
    )


def rope_angles(positions, head_size):
    half_size = head_size // 2
    freqs = ROPE_BASE ** (-(jnp.arange(half_size, dtype=F32) * 2.0 / head_size))
    angle = positions.astype(F32)[:, None] * freqs[None, :]
    return (jnp.cos(angle), jnp.sin(angle))


def rotate(values, cosine, sine_table, direction):
    half_size = values.shape[-1] // 2
    front_half = values[..., :half_size]
    back_half = values[..., half_size:]
    cos_wide = cosine[:, None, None, :]
    sin_wide = sine_table[:, None, None, :] * direction
    return jnp.concatenate(
        [
            front_half * cos_wide - back_half * sin_wide,
            back_half * cos_wide + front_half * sin_wide,
        ],
        axis=-1,
    )


def rms_scale(values):
    return lax.rsqrt(jnp.mean(values * values, axis=-1, keepdims=True) + NORM_EPSILON)


def norm_back(grad_norm, normed, inv_rms, gain_vec):
    scaled = grad_norm * gain_vec
    return inv_rms * (scaled - normed * jnp.mean(scaled * normed, axis=-1, keepdims=True))


def after(value, marker):
    return lax.optimization_barrier((value, marker))[0]


def make_local(sizes):
    fs, cs, ts = sizes["fsdp"], sizes["ctx"], sizes["tp"]
    assert fs == 4 and ts == 2

    def flip(value, axis, distance):
        return lax.ppermute(value, axis, [(i, i ^ distance) for i in range(sizes[axis])])

    def butterfly(value, axis, combine):
        distance = 1
        while distance < sizes[axis]:
            value = combine(value, flip(value, axis, distance))
            distance *= 2
        return value

    def gather_near(value):
        far = flip(value, "fsdp", 2)
        return [value, flip(value, "fsdp", 1), far, flip(far, "fsdp", 1)]

    def reduce_near(parts):
        near = flip(jnp.stack([parts[1], parts[3]]), "fsdp", 1)
        mine = parts[0].astype(F32) + near[0].astype(F32)
        other = (parts[2].astype(F32) + near[1].astype(F32)).astype(BF16)
        return mine.astype(F32) + flip(other, "fsdp", 2).astype(F32)

    def swap_near(block_of, f_index):
        sent = [block_of(f_index ^ d) for d in range(fs)]
        return [sent[0]] + [flip(sent[d], "fsdp", d) for d in range(1, fs)]

    def place(parts, f_index, axis, dtype=None):
        size = parts[0].shape[axis]
        shape = list(parts[0].shape)
        shape[axis] = size * fs
        out = jnp.zeros(shape, dtype or parts[0].dtype)
        for d in range(fs):
            out = lax.dynamic_update_slice_in_dim(
                out, parts[d].astype(out.dtype), (f_index ^ d) * size, axis
            )
        return out

    def tp_sum(value):
        low = value.astype(BF16)
        return low.astype(F32) + flip(low, "tp", 1).astype(F32)

    def line_sum(chunk_of, c_index):
        n = cs
        if n > 4:
            whole = jnp.stack([chunk_of(t) for t in range(n)])
            return lax.psum_scatter(whole, "ctx", scatter_dimension=0, tiled=False).astype(F32)
        total = chunk_of(c_index).astype(F32)
        for direction in (1, -1):
            got = None
            for s in range(1, n):
                if direction == 1:
                    pairs = [(i, i + 1) for i in range(s)]
                    index = c_index + (n - s)
                else:
                    pairs = [(n - 1 - i, n - 2 - i) for i in range(s)]
                    index = c_index - (n - s)
                sent = chunk_of(jnp.clip(index, 0, n - 1))
                if got is not None:
                    sent = (sent.astype(F32) + got.astype(F32)).astype(BF16)
                got = lax.ppermute(sent, "ctx", pairs)
            if got is not None:
                total = total + got.astype(F32)
        return total

    def line_spread(value, c_index, axis):
        n = cs
        if n > 4:
            whole = lax.all_gather(value, "ctx", axis=axis, tiled=False)
            return whole.astype(F32)
        right, left = [value], [value]
        for k in range(1, n):
            right.append(
                lax.ppermute(right[-1], "ctx", [(i, i + 1) for i in range(k - 1, n - 1)])
            )
            left.append(
                lax.ppermute(left[-1], "ctx", [(n - 1 - i, n - 2 - i) for i in range(k - 1, n - 1)])
            )
        shape = list(value.shape)
        shape.insert(axis, n)
        out = jnp.zeros(shape, F32)
        for k in range(n):
            if k == 0:
                piece = value.astype(F32)
            else:
                piece = right[k].astype(F32) + left[n - k].astype(F32)
            out = lax.dynamic_update_slice_in_dim(
                out, jnp.expand_dims(piece, axis), (c_index - k) % n, axis
            )
        return out

    def local(
        inputs,
        segments,
        norm_attn,
        query_weight,
        key_weight,
        value_weight,
        out_weight,
        norm_mlp,
        gate_weight,
        up_weight,
        down_weight,
        thresholds,
        cotangent,
    ):
        piece_len, seq_count, model_width = inputs.shape
        row_count = piece_len * seq_count
        f_index = lax.axis_index("fsdp")
        c_index = lax.axis_index("ctx")
        shard = model_width // fs
        q_cols = query_weight.shape[1]
        k_cols = key_weight.shape[1]
        heads_local = q_cols // HD
        groups_local = k_cols // HD
        group_size = heads_local // groups_local
        hidden_slice = gate_weight.shape[1] // fs
        full_len = piece_len * cs
        longest = full_len // 2
        back = min(cs - 1, (longest + piece_len - 2) // piece_len)
        shift_right = [(i, i + 1) for i in range(cs - 1)]
        shift_left = [(i + 1, i) for i in range(cs - 1)]

        qkv_parts = gather_near(jnp.concatenate([query_weight, key_weight, value_weight], axis=1))
        gains = place(
            gather_near(jnp.stack([norm_attn, norm_mlp])), f_index, 1
        ).astype(F32)
        gain_one = gains[0]
        gain_two = gains[1]
        out_parts = gather_near(after(out_weight, qkv_parts[2]))
        gate_in = after(gate_weight, out_parts[2])
        gate_parts = swap_near(
            lambda j: lax.dynamic_slice_in_dim(gate_in, j * hidden_slice, hidden_slice, 1), f_index
        )
        up_in = after(up_weight, gate_parts[3])
        up_parts = swap_near(
            lambda j: lax.dynamic_slice_in_dim(up_in, j * hidden_slice, hidden_slice, 1), f_index
        )
        grad_top = cotangent.astype(F32).reshape(row_count, model_width)
        grad_mlp = after((RESIDUAL * grad_top).astype(BF16), up_parts[3])
        grad_mlp_all = jnp.concatenate(gather_near(grad_mlp), axis=0)
        down_in = after(down_weight, grad_mlp_all)
        down_parts = swap_near(
            lambda j: lax.dynamic_slice_in_dim(down_in, j * hidden_slice, hidden_slice, 0), f_index
        )

        qkv_full = place(qkv_parts, f_index, 0)
        out_full = place(out_parts, f_index, 1)
        gate_full = place(gate_parts, f_index, 0)
        up_full = place(up_parts, f_index, 0)
        down_full = place(down_parts, f_index, 1)

        positions = c_index * piece_len + jnp.arange(piece_len, dtype=jnp.int32)
        cosine, sine_table = rope_angles(positions, HD)
        flat_in = inputs.astype(F32).reshape(row_count, model_width)
        scale_one = rms_scale(flat_in)
        normed_one = flat_in * scale_one
        hidden_one = (normed_one * gain_one).astype(BF16)
        qkv_lin = matmul_plain(hidden_one, qkv_full)
        value_vec = qkv_lin[:, q_cols + k_cols :].astype(BF16)
        queries = rotate(
            qkv_lin[:, :q_cols].reshape(piece_len, seq_count, heads_local, HD),
            cosine,
            sine_table,
            1.0,
        ).astype(BF16)
        key_rot = rotate(
            qkv_lin[:, q_cols : q_cols + k_cols].reshape(piece_len, seq_count, groups_local, HD),
            cosine,
            sine_table,
            1.0,
        ).astype(BF16)
        grouped_q = queries.reshape(piece_len, seq_count, groups_local, group_size, HD)
        kv_list = [
            jnp.stack(
                [key_rot, value_vec.reshape(piece_len, seq_count, groups_local, HD)]
            )
        ]
        seg_own = segments.T
        seg_list = [seg_own]
        for r in range(back):
            kv_list.append(lax.ppermute(kv_list[-1], "ctx", shift_right))
            seg_list.append(lax.ppermute(seg_list[-1], "ctx", shift_right))
        kv_all = jnp.concatenate(kv_list, axis=1)
        seg_all = jnp.concatenate(seg_list, axis=0)
        key_all, value_all = kv_all[0], kv_all[1]
        offsets = jnp.repeat(jnp.arange(back + 1, dtype=jnp.int32), piece_len)
        key_pos = jnp.tile(positions, back + 1) - offsets * piece_len
        allowed = (
            (seg_own[:, :, None] == seg_all.T[None, :, :])
            & (key_pos >= 0)[None, None, :]
            & ((positions // BLOCK)[:, None] >= (key_pos // BLOCK)[None, :])[:, None, :]
        )[:, :, None, None, :]
        scores = (
            jnp.einsum("cshgd,kshd->cshgk", grouped_q, key_all, preferred_element_type=F32)
            * ATTN_SCALE
        )
        masked = jnp.where(allowed, scores, NEG_FILL)
        run_peak = jnp.max(masked, axis=-1)
        weights_raw = jnp.exp(masked - run_peak[..., None])
        run_total = jnp.sum(weights_raw, axis=-1)
        out_f32 = (
            jnp.einsum(
                "cshgk,kshd->cshgd", weights_raw.astype(BF16), value_all, preferred_element_type=F32
            )
            / run_total[..., None]
        )
        log_total = run_peak + jnp.log(run_total)
        top_seen = jnp.max(run_peak, axis=(0, 1)).reshape(heads_local)
        head_peaks = butterfly(butterfly(top_seen, "fsdp", jnp.maximum), "ctx", jnp.maximum)
        attn_out = out_f32.reshape(row_count, heads_local * HD).astype(BF16)
        attn_sum = tp_sum(matmul_plain(attn_out, out_full))
        middle = flat_in + RESIDUAL * attn_sum
        scale_two = rms_scale(middle)
        normed_two = middle * scale_two
        hidden_two = (normed_two * gain_two).astype(BF16)

        hidden_all = jnp.concatenate(gather_near(hidden_two), axis=0)
        gate_val = matmul_plain(hidden_all, gate_full)
        up_val = matmul_plain(hidden_all, up_full)
        gate_sig = jax.nn.sigmoid(gate_val)
        activated = gate_val * gate_sig
        inner_act = (activated * up_val).astype(BF16)
        grad_inner = contract_cols(grad_mlp_all, down_full)
        grad_gate = (grad_inner * up_val * gate_sig * (1.0 + gate_val * (1.0 - gate_sig))).astype(
            BF16
        )
        grad_upv = (grad_inner * activated).astype(BF16)
        back_part = (contract_cols(grad_gate, gate_full) + contract_cols(grad_upv, up_full)).astype(
            BF16
        )
        back_part = back_part.reshape(fs, row_count, model_width)
        grad_hidden_two = tp_sum(reduce_near([back_part[d] for d in range(fs)]))

        rows_of = hidden_slice // cs
        d_rows = shard // cs
        down_grad = contract_rows(inner_act, grad_mlp_all).astype(BF16)
        gate_grad = contract_rows(hidden_all, grad_gate).astype(BF16)
        up_grad = contract_rows(hidden_all, grad_upv).astype(BF16)

        def own_down(grad):
            grad = grad.reshape(cs, rows_of, model_width)
            chunk = line_sum(
                lambda t: lax.dynamic_index_in_dim(grad, t, 0, keepdims=False), c_index
            ).astype(BF16)
            parts = swap_near(
                lambda j: lax.dynamic_slice_in_dim(chunk, j * shard, shard, 1), f_index
            )
            chunk = place([part[None] for part in parts], f_index, 0)
            return line_spread(chunk, c_index, 1).reshape(fs * hidden_slice, shard)

        def own_wide(grad):
            grad = grad.reshape(fs, cs, d_rows, hidden_slice)
            chunk = line_sum(
                lambda t: lax.dynamic_index_in_dim(grad, t, 1, keepdims=False), c_index
            ).astype(BF16)
            parts = swap_near(
                lambda j: lax.dynamic_index_in_dim(chunk, j, 0, keepdims=False), f_index
            )
            chunk = place(parts, f_index, 1)
            return line_spread(chunk, c_index, 0).reshape(shard, fs * hidden_slice)

        def own_rows(value):
            rows, cols = value.shape
            value = value.astype(BF16).reshape(cs, rows // cs, cols)
            chunk = line_sum(
                lambda t: lax.dynamic_index_in_dim(value, t, 0, keepdims=False), c_index
            ).astype(BF16)
            return line_spread(chunk, c_index, 0).reshape(rows, cols)

        grad_down_w = own_down(down_grad)
        grad_gate_w = own_wide(gate_grad)
        grad_up_w = own_wide(up_grad)

        mlp_part = matmul_plain(inner_act, down_full).astype(BF16)
        mlp_part = mlp_part.reshape(fs, row_count, model_width)
        mlp_sum = tp_sum(reduce_near([mlp_part[d] for d in range(fs)]))
        output = (
            (middle + RESIDUAL * mlp_sum).astype(BF16).reshape(piece_len, seq_count, model_width)
        )

        grad_gain_mlp = jnp.sum(grad_hidden_two * normed_two, axis=0)
        grad_middle = grad_top + norm_back(grad_hidden_two, normed_two, scale_two, gain_two)
        grad_attn = (RESIDUAL * grad_middle).astype(BF16)
        grad_heads = (
            contract_cols(grad_attn, out_full)
            .astype(BF16)
            .reshape(piece_len, seq_count, groups_local, group_size, HD)
        )
        out_grad = contract_rows(attn_out, grad_attn).astype(BF16)
        grad_out_w = own_rows(
            reduce_near(
                [
                    lax.dynamic_slice_in_dim(out_grad, (f_index ^ d) * shard, shard, 1)
                    for d in range(fs)
                ]
            )
        )
        row_dot = jnp.sum(grad_heads.astype(F32) * out_f32, axis=-1)
        weights_now = jnp.exp(masked - log_total[..., None])
        grad_values = jnp.einsum(
            "cshgk,cshgd->kshd", weights_now.astype(BF16), grad_heads, preferred_element_type=F32
        )
        grad_weights = jnp.einsum(
            "cshgd,kshd->cshgk", grad_heads, value_all, preferred_element_type=F32
        )
        grad_scores = (weights_now * (grad_weights - row_dot[..., None])).astype(BF16)
        grad_query = (
            jnp.einsum("cshgk,kshd->cshgd", grad_scores, key_all, preferred_element_type=F32)
            * ATTN_SCALE
        )
        grad_keys = (
            jnp.einsum("cshgk,cshgd->kshd", grad_scores, grouped_q, preferred_element_type=F32)
            * ATTN_SCALE
        )
        kv_grad = jnp.stack([grad_keys, grad_values]).reshape(
            2, back + 1, piece_len, seq_count, groups_local, HD
        )
        carried = None
        for r in range(back, 0, -1):
            sent = kv_grad[:, r]
            if carried is not None:
                sent = sent + carried.astype(F32)
            carried = lax.ppermute(sent.astype(BF16), "ctx", shift_left)
        kv_own = kv_grad[:, 0]
        if carried is not None:
            kv_own = kv_own + carried.astype(F32)
        grad_query_lin = rotate(
            grad_query.reshape(piece_len, seq_count, heads_local, HD), cosine, sine_table, -1.0
        ).reshape(row_count, q_cols)
        grad_key_lin = rotate(kv_own[0], cosine, sine_table, -1.0).reshape(row_count, k_cols)
        grad_qkv_lin = jnp.concatenate(
            [
                grad_query_lin.astype(BF16),
                grad_key_lin.astype(BF16),
                kv_own[1].reshape(row_count, k_cols).astype(BF16),
            ],
            axis=1,
        )
        qkv_grad = contract_rows(hidden_one, grad_qkv_lin).astype(BF16)
        qkv_own = own_rows(
            reduce_near(
                [
                    lax.dynamic_slice_in_dim(qkv_grad, (f_index ^ d) * shard, shard, 0)
                    for d in range(fs)
                ]
            )
        )
        grad_hidden_one = tp_sum(contract_cols(grad_qkv_lin, qkv_full))
        grad_gain_attn = jnp.sum(grad_hidden_one * normed_one, axis=0)
        input_grad = (
            grad_middle + norm_back(grad_hidden_one, normed_one, scale_one, gain_one)
        ).reshape(piece_len, seq_count, model_width)
        gain_sums = butterfly(
            butterfly(jnp.stack([grad_gain_attn, grad_gain_mlp]), "fsdp", jnp.add), "ctx", jnp.add
        )
        gain_own = lax.dynamic_slice_in_dim(gain_sums, f_index * shard, shard, 1)

        ratio_clip = thresholds / jnp.maximum(head_peaks, thresholds)
        query_factor = jnp.repeat(jnp.sqrt(ratio_clip), HD)
        key_factor = jnp.repeat(
            jnp.sqrt(jnp.min(ratio_clip.reshape(groups_local, group_size), axis=1)), HD
        )
        clipped_query = (query_weight.astype(F32) * query_factor[None, :]).astype(BF16)
        clipped_key = (key_weight.astype(F32) * key_factor[None, :]).astype(BF16)
        return (
            output,
            input_grad,
            gain_own[0],
            qkv_own[:, :q_cols],
            qkv_own[:, q_cols : q_cols + k_cols],
            qkv_own[:, q_cols + k_cols :],
            grad_out_w,
            gain_own[1],
            grad_gate_w,
            grad_up_w,
            grad_down_w,
            head_peaks,
            clipped_query,
            clipped_key,
        )

    return local


def solution(mesh):
    placed = (
        P("ctx", "fsdp", None),
        P("fsdp", "ctx"),
        P("fsdp"),
        P("fsdp", "tp"),
        P("fsdp", "tp"),
        P("fsdp", "tp"),
        P("tp", "fsdp"),
        P("fsdp"),
        P("fsdp", "tp"),
        P("fsdp", "tp"),
        P("tp", "fsdp"),
        P("tp"),
        P("ctx", "fsdp", None),
    )
    return jax.shard_map(
        make_local({name: mesh.shape[name] for name in ("fsdp", "ctx", "tp")}),
        mesh=mesh,
        in_specs=placed,
        out_specs=(
            P("ctx", "fsdp", None),
            P("ctx", "fsdp", None),
            P("fsdp"),
            P("fsdp", "tp"),
            P("fsdp", "tp"),
            P("fsdp", "tp"),
            P("tp", "fsdp"),
            P("fsdp"),
            P("fsdp", "tp"),
            P("fsdp", "tp"),
            P("tp", "fsdp"),
            P("tp"),
            P("fsdp", "tp"),
            P("fsdp", "tp"),
        ),
        check_vma=False,
    )
```

```python
import jax
import jax.numpy as jnp
from jax import lax
from jax.sharding import PartitionSpec as P

HD = 64
BLOCK = 256

NORM_EPSILON = 1e-05
ROPE_BASE = 10000000.0
RESIDUAL = 0.22
ATTN_SCALE = 1.0 / 64.0
NEG_FILL = -1e30


F32 = jnp.float32
BF16 = jnp.bfloat16


def matmul_plain(left_mat, right_mat):
    return jnp.dot(left_mat, right_mat, preferred_element_type=F32)


def contract_rows(left_mat, right_mat):
    return lax.dot_general(
        left_mat, right_mat, (((0,), (0,)), ((), ())), preferred_element_type=F32
    )


def contract_cols(left_mat, right_mat):
    return lax.dot_general(
        left_mat, right_mat, (((1,), (1,)), ((), ())), preferred_element_type=F32
    )


def rope_angles(positions, head_size):
    half_size = head_size // 2
    freqs = ROPE_BASE ** (-(jnp.arange(half_size, dtype=F32) * 2.0 / head_size))
    angle = positions.astype(F32)[:, None] * freqs[None, :]
    return (jnp.cos(angle), jnp.sin(angle))


def rotate(values, cosine, sine_table, direction):
    half_size = values.shape[-1] // 2
    front_half = values[..., :half_size]
    back_half = values[..., half_size:]
    cos_wide = cosine[:, None, None, :]
    sin_wide = sine_table[:, None, None, :] * direction
    return jnp.concatenate(
        [
            front_half * cos_wide - back_half * sin_wide,
            back_half * cos_wide + front_half * sin_wide,
        ],
        axis=-1,
    )


def rms_scale(values):
    return lax.rsqrt(jnp.mean(values * values, axis=-1, keepdims=True) + NORM_EPSILON)


def norm_back(grad_norm, normed, inv_rms, gain_vec):
    scaled = grad_norm * gain_vec
    return inv_rms * (scaled - normed * jnp.mean(scaled * normed, axis=-1, keepdims=True))


def after(value, marker):
    return lax.optimization_barrier((value, marker))[0]


def make_local(sizes):
    fs, cs, ts = sizes["fsdp"], sizes["ctx"], sizes["tp"]
    assert fs == 4 and ts == 2 and cs % 2 == 0

    def flip(value, axis, distance):
        return lax.ppermute(value, axis, [(i, i ^ distance) for i in range(sizes[axis])])

    def butterfly(value, axis, combine):
        distance = 1
        while distance < sizes[axis]:
            value = combine(value, flip(value, axis, distance))
            distance *= 2
        return value

    def gather_near(value):
        far = flip(value, "fsdp", 2)
        return [value, flip(value, "fsdp", 1), far, flip(far, "fsdp", 1)]

    def cross(half_of, c_index, axis, hold=None):
        which = c_index % 2
        got = flip(half_of(which), "fsdp", 2)
        mark = got
        if hold is not None:
            got = after(got, hold)
        other = flip(got, "ctx", 1)
        first = which == 0
        whole = jnp.concatenate(
            [jnp.where(first, got, other), jnp.where(first, other, got)], axis=axis
        )
        return whole, mark

    def gather_shared(value, c_index, hold):
        rows = value.shape[0] // 2
        far, mark = cross(
            lambda h: lax.dynamic_slice_in_dim(value, h * rows, rows, 0), c_index, 0, hold
        )
        return [value, flip(value, "fsdp", 1), far, flip(far, "fsdp", 1)], mark

    def swap_shared(block_of, rows, f_index, c_index, hold, near_hold):
        half = rows // 2
        far, mark = cross(
            lambda h: jnp.stack([block_of(f_index ^ d, h * half, half) for d in (2, 3)]),
            c_index,
            1,
            hold,
        )
        far = after(far, near_hold)
        near = flip(jnp.stack([block_of(f_index ^ 1, 0, rows), far[1]]), "fsdp", 1)
        return [block_of(f_index, 0, rows), near[0], far[0], near[1]], mark

    def reduce_near(parts):
        near = flip(jnp.stack([parts[1], parts[3]]), "fsdp", 1)
        mine = parts[0].astype(F32) + near[0].astype(F32)
        other = (parts[2].astype(F32) + near[1].astype(F32)).astype(BF16)
        return mine.astype(F32) + flip(other, "fsdp", 2).astype(F32)

    def swap_near(block_of, f_index):
        sent = [block_of(f_index ^ d) for d in range(fs)]
        return [sent[0]] + [flip(sent[d], "fsdp", d) for d in range(1, fs)]

    def place(parts, f_index, axis, dtype=None):
        size = parts[0].shape[axis]
        shape = list(parts[0].shape)
        shape[axis] = size * fs
        out = jnp.zeros(shape, dtype or parts[0].dtype)
        for d in range(fs):
            out = lax.dynamic_update_slice_in_dim(
                out, parts[d].astype(out.dtype), (f_index ^ d) * size, axis
            )
        return out

    def tp_sum(value):
        low = value.astype(BF16)
        return low.astype(F32) + flip(low, "tp", 1).astype(F32)

    def line_total(value, c_index, box, mid=None, axis=0):
        n = cs
        rows, cols = value.shape
        chunks = value.astype(BF16).reshape(n, rows // n, cols)

        def chunk_of(t):
            return lax.dynamic_index_in_dim(chunks, jnp.clip(t, 0, n - 1), 0, keepdims=False)

        hold = yield None
        got = {}
        for s in range(1, n):
            pairs = {
                1: [(i, i + 1) for i in range(s)],
                -1: [(n - 1 - i, n - 2 - i) for i in range(s)],
            }
            for way in (1, -1):
                sent = chunk_of(c_index + way * (n - s))
                if way in got:
                    sent = (sent.astype(F32) + got[way].astype(F32)).astype(BF16)
                got[way] = lax.ppermute(hold(sent), "ctx", pairs[way])
            hold = yield tuple(got.values())
        total = chunk_of(c_index).astype(F32)
        for way in got:
            total = total + got[way].astype(F32)
        own = total.astype(BF16)
        if mid is not None:
            own = mid(own)
        right, left = [own], [own]
        for k in range(1, n):
            right.append(
                lax.ppermute(hold(right[-1]), "ctx", [(i, i + 1) for i in range(k - 1, n - 1)])
            )
            left.append(
                lax.ppermute(
                    hold(left[-1]), "ctx", [(n - 1 - i, n - 2 - i) for i in range(k - 1, n - 1)]
                )
            )
            hold = yield (right[-1], left[-1])
        shape = list(own.shape)
        shape.insert(axis, n)
        out = jnp.zeros(shape, F32)
        for k in range(n):
            if k == 0:
                piece = own.astype(F32)
            else:
                piece = right[k].astype(F32) + left[n - k].astype(F32)
            out = lax.dynamic_update_slice_in_dim(
                out, jnp.expand_dims(piece, axis), (c_index - k) % n, axis
            )
        box.append(out)

    def butterfly_steps(value, combine, axes, box):
        hold = yield None
        for axis in axes:
            distance = 1
            while distance < sizes[axis]:
                got = flip(hold(value), axis, distance)
                value = combine(value, got)
                distance *= 2
                hold = yield (got,)
        box.append(value)

    def run_steps(jobs):
        live = []
        for first, job in jobs:
            next(job)
            live.append((first, job))
        step, marker = 1, None
        while live:
            seen, rest = [], []
            held = marker
            hold = (lambda x: after(x, held)) if held else (lambda x: x)
            for first, job in live:
                if first > step:
                    rest.append((first, job))
                    continue
                try:
                    seen.extend(job.send(hold))
                    rest.append((first, job))
                except StopIteration:
                    pass
            live, marker, step = rest, tuple(seen), step + 1

    def local(
        inputs,
        segments,
        norm_attn,
        query_weight,
        key_weight,
        value_weight,
        out_weight,
        norm_mlp,
        gate_weight,
        up_weight,
        down_weight,
        thresholds,
        cotangent,
    ):
        piece_len, seq_count, model_width = inputs.shape
        row_count = piece_len * seq_count
        f_index = lax.axis_index("fsdp")
        c_index = lax.axis_index("ctx")
        shard = model_width // fs
        q_cols = query_weight.shape[1]
        k_cols = key_weight.shape[1]
        heads_local = q_cols // HD
        groups_local = k_cols // HD
        group_size = heads_local // groups_local
        hidden_slice = gate_weight.shape[1] // fs
        full_len = piece_len * cs
        longest = full_len // 2
        back = min(cs - 1, (longest + piece_len - 2) // piece_len)
        shift_right = [(i, i + 1) for i in range(cs - 1)]
        shift_left = [(i + 1, i) for i in range(cs - 1)]

        qkv_parts = gather_near(jnp.concatenate([query_weight, key_weight, value_weight], axis=1))
        gains = place(
            gather_near(jnp.stack([norm_attn, norm_mlp])), f_index, 1
        ).astype(F32)
        gain_one = gains[0]
        gain_two = gains[1]
        qkv_full = place(qkv_parts, f_index, 0)
        positions = c_index * piece_len + jnp.arange(piece_len, dtype=jnp.int32)
        cosine, sine_table = rope_angles(positions, HD)
        flat_in = inputs.astype(F32).reshape(row_count, model_width)
        scale_one = rms_scale(flat_in)
        normed_one = flat_in * scale_one
        hidden_one = (normed_one * gain_one).astype(BF16)
        qkv_lin = matmul_plain(hidden_one, qkv_full)
        out_parts, _ = gather_shared(after(out_weight, qkv_parts[1]), c_index, qkv_lin)
        grad_top = cotangent.astype(F32).reshape(row_count, model_width)
        grad_mlp = after((RESIDUAL * grad_top).astype(BF16), qkv_lin)
        grad_mlp_all = jnp.concatenate(gather_near(grad_mlp), axis=0)
        value_vec = qkv_lin[:, q_cols + k_cols :].astype(BF16)
        queries = rotate(
            qkv_lin[:, :q_cols].reshape(piece_len, seq_count, heads_local, HD),
            cosine,
            sine_table,
            1.0,
        ).astype(BF16)
        key_rot = rotate(
            qkv_lin[:, q_cols : q_cols + k_cols].reshape(piece_len, seq_count, groups_local, HD),
            cosine,
            sine_table,
            1.0,
        ).astype(BF16)
        grouped_q = queries.reshape(piece_len, seq_count, groups_local, group_size, HD)
        kv_list = [
            jnp.stack(
                [key_rot, value_vec.reshape(piece_len, seq_count, groups_local, HD)]
            )
        ]
        seg_own = segments.T
        seg_list = [seg_own]
        for r in range(back):
            kv_list.append(lax.ppermute(kv_list[-1], "ctx", shift_right))
            seg_list.append(lax.ppermute(seg_list[-1], "ctx", shift_right))
        kv_all = jnp.concatenate(kv_list, axis=1)
        seg_all = jnp.concatenate(seg_list, axis=0)
        key_all, value_all = kv_all[0], kv_all[1]
        offsets = jnp.repeat(jnp.arange(back + 1, dtype=jnp.int32), piece_len)
        key_pos = jnp.tile(positions, back + 1) - offsets * piece_len
        allowed = (
            (seg_own[:, :, None] == seg_all.T[None, :, :])
            & (key_pos >= 0)[None, None, :]
            & ((positions // BLOCK)[:, None] >= (key_pos // BLOCK)[None, :])[:, None, :]
        )[:, :, None, None, :]
        scores = (
            jnp.einsum("cshgd,kshd->cshgk", grouped_q, key_all, preferred_element_type=F32)
            * ATTN_SCALE
        )
        masked = jnp.where(allowed, scores, NEG_FILL)
        run_peak = jnp.max(masked, axis=-1)
        weights_raw = jnp.exp(masked - run_peak[..., None])
        run_total = jnp.sum(weights_raw, axis=-1)
        out_f32 = (
            jnp.einsum(
                "cshgk,kshd->cshgd", weights_raw.astype(BF16), value_all, preferred_element_type=F32
            )
            / run_total[..., None]
        )
        log_total = run_peak + jnp.log(run_total)
        top_seen = jnp.max(run_peak, axis=(0, 1)).reshape(heads_local)
        out_full = place(out_parts, f_index, 1)
        attn_out = out_f32.reshape(row_count, heads_local * HD).astype(BF16)
        att_part = matmul_plain(attn_out, out_full).astype(BF16)
        gate_in, up_in = lax.optimization_barrier((gate_weight, up_weight, out_parts[1]))[:2]

        def gate_up_block(j, first, rows):
            start = (first, j * hidden_slice)
            return jnp.concatenate(
                [
                    lax.dynamic_slice(gate_in, start, (rows, hidden_slice)),
                    lax.dynamic_slice(up_in, start, (rows, hidden_slice)),
                ],
                axis=1,
            )

        gate_up_parts, _ = swap_shared(gate_up_block, shard, f_index, c_index, kv_list[-1], att_part)
        down_in = after(down_weight, qkv_lin)
        down_parts, _ = swap_shared(
            lambda j, first, rows: lax.dynamic_slice_in_dim(
                down_in, j * hidden_slice + first, rows, 0
            ),
            hidden_slice,
            f_index,
            c_index,
            out_f32,
            att_part,
        )

        gate_up_full = place(gate_up_parts, f_index, 0)
        down_full = place(down_parts, f_index, 1)
        attn_sum = tp_sum(att_part)
        middle = flat_in + RESIDUAL * attn_sum
        scale_two = rms_scale(middle)
        normed_two = middle * scale_two
        hidden_two = (normed_two * gain_two).astype(BF16)

        def own_wide(grad):
            parts = swap_near(
                lambda j: lax.dynamic_slice_in_dim(grad, j * shard, shard, 0), f_index
            )
            return place(parts, f_index, 1)

        hidden_all = jnp.concatenate(gather_near(hidden_two), axis=0)
        gate_up_val = matmul_plain(hidden_all, gate_up_full)
        gate_val = gate_up_val[:, :hidden_slice]
        up_val = gate_up_val[:, hidden_slice:]
        gate_sig = jax.nn.sigmoid(gate_val)
        activated = gate_val * gate_sig
        inner_act = (activated * up_val).astype(BF16)
        grad_inner = contract_cols(grad_mlp_all, down_full)
        grad_gate = (grad_inner * up_val * gate_sig * (1.0 + gate_val * (1.0 - gate_sig))).astype(
            BF16
        )
        grad_upv = (grad_inner * activated).astype(BF16)
        grad_gate_up = jnp.concatenate([grad_gate, grad_upv], axis=1)
        back_part = contract_cols(grad_gate_up, gate_up_full).astype(BF16)
        back_part = back_part.reshape(fs, row_count, model_width)
        hidden_two_sum = reduce_near([back_part[d] for d in range(fs)])
        grad_hidden_two = tp_sum(hidden_two_sum)

        down_grad = contract_rows(inner_act, grad_mlp_all).astype(BF16)
        gate_grad = contract_rows(hidden_all, grad_gate).astype(BF16)
        up_grad = contract_rows(hidden_all, grad_upv).astype(BF16)
        gate_own = own_wide(after(gate_grad, hidden_two_sum))
        up_own = own_wide(after(up_grad, gate_own))

        mlp_part = matmul_plain(inner_act, down_full).astype(BF16)
        mlp_part = mlp_part.reshape(fs, row_count, model_width)
        mlp_sum = tp_sum(reduce_near([mlp_part[d] for d in range(fs)]))
        output = (
            (middle + RESIDUAL * mlp_sum).astype(BF16).reshape(piece_len, seq_count, model_width)
        )

        grad_gain_mlp = jnp.sum(grad_hidden_two * normed_two, axis=0)
        grad_middle = grad_top + norm_back(grad_hidden_two, normed_two, scale_two, gain_two)
        grad_attn = (RESIDUAL * grad_middle).astype(BF16)
        grad_heads = (
            contract_cols(grad_attn, out_full)
            .astype(BF16)
            .reshape(piece_len, seq_count, groups_local, group_size, HD)
        )
        out_grad = contract_rows(attn_out, grad_attn).astype(BF16)
        out_own = (
            reduce_near(
                [
                    lax.dynamic_slice_in_dim(out_grad, (f_index ^ d) * shard, shard, 1)
                    for d in range(fs)
                ]
            )
        )
        row_dot = jnp.sum(grad_heads.astype(F32) * out_f32, axis=-1)
        weights_now = jnp.exp(masked - log_total[..., None])
        grad_values = jnp.einsum(
            "cshgk,cshgd->kshd", weights_now.astype(BF16), grad_heads, preferred_element_type=F32
        )
        grad_weights = jnp.einsum(
            "cshgd,kshd->cshgk", grad_heads, value_all, preferred_element_type=F32
        )
        grad_scores = (weights_now * (grad_weights - row_dot[..., None])).astype(BF16)
        grad_query = (
            jnp.einsum("cshgk,kshd->cshgd", grad_scores, key_all, preferred_element_type=F32)
            * ATTN_SCALE
        )
        grad_keys = (
            jnp.einsum("cshgk,cshgd->kshd", grad_scores, grouped_q, preferred_element_type=F32)
            * ATTN_SCALE
        )
        kv_grad = jnp.stack([grad_keys, grad_values]).reshape(
            2, back + 1, piece_len, seq_count, groups_local, HD
        )
        carried = None
        for r in range(back, 0, -1):
            sent = kv_grad[:, r]
            if carried is not None:
                sent = sent + carried.astype(F32)
            carried = lax.ppermute(sent.astype(BF16), "ctx", shift_left)
        kv_own = kv_grad[:, 0]
        if carried is not None:
            kv_own = kv_own + carried.astype(F32)
        grad_query_lin = rotate(
            grad_query.reshape(piece_len, seq_count, heads_local, HD), cosine, sine_table, -1.0
        ).reshape(row_count, q_cols)
        grad_key_lin = rotate(kv_own[0], cosine, sine_table, -1.0).reshape(row_count, k_cols)
        grad_qkv_lin = jnp.concatenate(
            [
                grad_query_lin.astype(BF16),
                grad_key_lin.astype(BF16),
                kv_own[1].reshape(row_count, k_cols).astype(BF16),
            ],
            axis=1,
        )
        qkv_grad = contract_rows(hidden_one, grad_qkv_lin).astype(BF16)
        qkv_sum = (
            reduce_near(
                [
                    lax.dynamic_slice_in_dim(qkv_grad, (f_index ^ d) * shard, shard, 0)
                    for d in range(fs)
                ]
            )
        )
        grad_hidden_one = tp_sum(contract_cols(grad_qkv_lin, qkv_full))
        grad_gain_attn = jnp.sum(grad_hidden_one * normed_one, axis=0)
        input_grad = (
            grad_middle + norm_back(grad_hidden_one, normed_one, scale_one, gain_one)
        ).reshape(piece_len, seq_count, model_width)
        gain_fsdp = butterfly(jnp.stack([grad_gain_attn, grad_gain_mlp]), "fsdp", jnp.add)
        gain_fsdp = lax.dynamic_slice_in_dim(gain_fsdp, f_index * shard, shard, 1)

        def down_mid(low):
            parts = swap_near(
                lambda j: lax.dynamic_slice_in_dim(low, j * shard, shard, 1), f_index
            )
            return place([part[None] for part in parts], f_index, 0)

        boxes = [[] for _ in range(7)]
        units = (down_grad, gate_own, up_own, out_own, qkv_sum)
        if cs > 4:
            for box, unit in zip(boxes, units):
                part = lax.psum_scatter(
                    unit.astype(BF16), "ctx", scatter_dimension=0, tiled=True
                )
                axis = 0
                if unit is down_grad:
                    part, axis = down_mid(part), 1
                box.append(lax.all_gather(part, "ctx", axis=axis, tiled=False).astype(F32))
            boxes[5].append(butterfly(butterfly(top_seen, "fsdp", jnp.maximum), "ctx", jnp.maximum))
            boxes[6].append(butterfly(gain_fsdp, "ctx", jnp.add))
        else:
            jobs = [(1, line_total(down_grad, c_index, boxes[0], down_mid, 1))]
            starts = (1 + cs, 1 + 2 * cs, 2 + cs, 2 + 2 * cs)
            for first, unit, box in zip(starts, units[1:], boxes[1:5]):
                jobs.append((first, line_total(unit, c_index, box)))
            jobs.append(
                (2 + 2 * cs, butterfly_steps(top_seen, jnp.maximum, ("fsdp", "ctx"), boxes[5]))
            )
            jobs.append((5 + 2 * cs, butterfly_steps(gain_fsdp, jnp.add, ("ctx",), boxes[6])))
            run_steps(jobs)
        (down_all,), (gate_all,), (up_all,), (out_all,), (qkv_all,) = boxes[:5]
        (head_peaks,), (gain_own,) = boxes[5:]
        grad_down_w = down_all.reshape(-1, shard)
        grad_gate_w = gate_all.reshape(shard, -1)
        grad_up_w = up_all.reshape(shard, -1)
        grad_out_w = out_all.reshape(-1, shard)
        qkv_own = qkv_all.reshape(shard, -1)

        ratio_clip = thresholds / jnp.maximum(head_peaks, thresholds)
        query_factor = jnp.repeat(jnp.sqrt(ratio_clip), HD)
        key_factor = jnp.repeat(
            jnp.sqrt(jnp.min(ratio_clip.reshape(groups_local, group_size), axis=1)), HD
        )
        clipped_query = (query_weight.astype(F32) * query_factor[None, :]).astype(BF16)
        clipped_key = (key_weight.astype(F32) * key_factor[None, :]).astype(BF16)
        return (
            output,
            input_grad,
            gain_own[0],
            qkv_own[:, :q_cols],
            qkv_own[:, q_cols : q_cols + k_cols],
            qkv_own[:, q_cols + k_cols :],
            grad_out_w,
            gain_own[1],
            grad_gate_w,
            grad_up_w,
            grad_down_w,
            head_peaks,
            clipped_query,
            clipped_key,
        )

    return local


def solution(mesh):
    placed = (
        P("ctx", "fsdp", None),
        P("fsdp", "ctx"),
        P("fsdp"),
        P("fsdp", "tp"),
        P("fsdp", "tp"),
        P("fsdp", "tp"),
        P("tp", "fsdp"),
        P("fsdp"),
        P("fsdp", "tp"),
        P("fsdp", "tp"),
        P("tp", "fsdp"),
        P("tp"),
        P("ctx", "fsdp", None),
    )
    return jax.shard_map(
        make_local({name: mesh.shape[name] for name in ("fsdp", "ctx", "tp")}),
        mesh=mesh,
        in_specs=placed,
        out_specs=(
            P("ctx", "fsdp", None),
            P("ctx", "fsdp", None),
            P("fsdp"),
            P("fsdp", "tp"),
            P("fsdp", "tp"),
            P("fsdp", "tp"),
            P("tp", "fsdp"),
            P("fsdp"),
            P("fsdp", "tp"),
            P("fsdp", "tp"),
            P("tp", "fsdp"),
            P("tp"),
            P("fsdp", "tp"),
            P("fsdp", "tp"),
        ),
        check_vma=False,
    )
```

```python
import jax
import jax.numpy as jnp
from jax import lax
from jax.sharding import PartitionSpec as P

HD = 64
BLOCK = 256

NORM_EPSILON = 1e-05
ROPE_BASE = 10000000.0
RESIDUAL = 0.22
ATTN_SCALE = 1.0 / 64.0
NEG_FILL = -1e30


F32 = jnp.float32
BF16 = jnp.bfloat16


def matmul_plain(left_mat, right_mat):
    return jnp.dot(left_mat, right_mat, preferred_element_type=F32)


def contract_rows(left_mat, right_mat):
    return lax.dot_general(
        left_mat, right_mat, (((0,), (0,)), ((), ())), preferred_element_type=F32
    )


def contract_cols(left_mat, right_mat):
    return lax.dot_general(
        left_mat, right_mat, (((1,), (1,)), ((), ())), preferred_element_type=F32
    )


def rope_angles(positions, head_size):
    half_size = head_size // 2
    freqs = ROPE_BASE ** (-(jnp.arange(half_size, dtype=F32) * 2.0 / head_size))
    angle = positions.astype(F32)[:, None] * freqs[None, :]
    return (jnp.cos(angle), jnp.sin(angle))


def rotate(values, cosine, sine_table, direction):
    half_size = values.shape[-1] // 2
    front_half = values[..., :half_size]
    back_half = values[..., half_size:]
    cos_wide = cosine[:, None, None, :]
    sin_wide = sine_table[:, None, None, :] * direction
    return jnp.concatenate(
        [
            front_half * cos_wide - back_half * sin_wide,
            back_half * cos_wide + front_half * sin_wide,
        ],
        axis=-1,
    )


def rms_scale(values):
    return lax.rsqrt(jnp.mean(values * values, axis=-1, keepdims=True) + NORM_EPSILON)


def norm_back(grad_norm, normed, inv_rms, gain_vec):
    scaled = grad_norm * gain_vec
    return inv_rms * (scaled - normed * jnp.mean(scaled * normed, axis=-1, keepdims=True))


def after(value, marker):
    return lax.optimization_barrier((value, marker))[0]


def make_local(sizes):
    fs, cs, ts = sizes["fsdp"], sizes["ctx"], sizes["tp"]
    assert fs == 4 and ts == 2 and cs % 2 == 0

    def flip(value, axis, distance):
        return lax.ppermute(value, axis, [(i, i ^ distance) for i in range(sizes[axis])])

    def butterfly(value, axis, combine):
        distance = 1
        while distance < sizes[axis]:
            value = combine(value, flip(value, axis, distance))
            distance *= 2
        return value

    def gather_near(value):
        far = flip(value, "fsdp", 2)
        return [value, flip(value, "fsdp", 1), far, flip(far, "fsdp", 1)]

    def cross(half_of, c_index, axis, hold=None):
        which = c_index % 2
        got = flip(half_of(which), "fsdp", 2)
        mark = got
        if hold is not None:
            got = after(got, hold)
        other = flip(got, "ctx", 1)
        first = which == 0
        whole = jnp.concatenate(
            [jnp.where(first, got, other), jnp.where(first, other, got)], axis=axis
        )
        return whole, mark

    def gather_shared(value, c_index, hold):
        rows = value.shape[0] // 2
        far, mark = cross(
            lambda h: lax.dynamic_slice_in_dim(value, h * rows, rows, 0), c_index, 0, hold
        )
        return [value, flip(value, "fsdp", 1), far, flip(far, "fsdp", 1)], mark

    def swap_shared(block_of, rows, f_index, c_index, hold, near_hold):
        half = rows // 2
        far, mark = cross(
            lambda h: jnp.stack([block_of(f_index ^ d, h * half, half) for d in (2, 3)]),
            c_index,
            1,
            hold,
        )
        far = after(far, near_hold)
        near = flip(jnp.stack([block_of(f_index ^ 1, 0, rows), far[1]]), "fsdp", 1)
        return [block_of(f_index, 0, rows), near[0], far[0], near[1]], mark

    def reduce_near(parts):
        near = flip(jnp.stack([parts[1], parts[3]]), "fsdp", 1)
        mine = parts[0].astype(F32) + near[0].astype(F32)
        other = (parts[2].astype(F32) + near[1].astype(F32)).astype(BF16)
        return mine.astype(F32) + flip(other, "fsdp", 2).astype(F32)

    def swap_near(block_of, f_index):
        sent = [block_of(f_index ^ d) for d in range(fs)]
        return [sent[0]] + [flip(sent[d], "fsdp", d) for d in range(1, fs)]

    def place(parts, f_index, axis, dtype=None):
        size = parts[0].shape[axis]
        shape = list(parts[0].shape)
        shape[axis] = size * fs
        out = jnp.zeros(shape, dtype or parts[0].dtype)
        for d in range(fs):
            out = lax.dynamic_update_slice_in_dim(
                out, parts[d].astype(out.dtype), (f_index ^ d) * size, axis
            )
        return out

    def tp_sum(value):
        low = value.astype(BF16)
        return low.astype(F32) + flip(low, "tp", 1).astype(F32)

    def line_total(value, c_index, box, mid=None, axis=0):
        hold = yield None
        n = cs
        if callable(value):
            value = value()
        if value.ndim == 2:
            value = value.astype(BF16).reshape(n, -1, value.shape[1])
        along = value.ndim - 3

        def chunk_of(t):
            return lax.dynamic_index_in_dim(value, jnp.clip(t, 0, n - 1), along, keepdims=False)

        got = {}
        for s in range(1, n):
            pairs = {
                1: [(i, i + 1) for i in range(s)],
                -1: [(n - 1 - i, n - 2 - i) for i in range(s)],
            }
            for way in (1, -1):
                sent = chunk_of(c_index + way * (n - s))
                if way in got:
                    sent = (sent.astype(F32) + got[way].astype(F32)).astype(BF16)
                got[way] = lax.ppermute(hold(sent), "ctx", pairs[way])
            hold = yield tuple(got.values())
        total = chunk_of(c_index).astype(F32)
        for way in got:
            total = total + got[way].astype(F32)
        own = total.astype(BF16)
        if mid is not None:
            own = mid(own)
        right, left = [own], [own]
        for k in range(1, n):
            right.append(
                lax.ppermute(hold(right[-1]), "ctx", [(i, i + 1) for i in range(k - 1, n - 1)])
            )
            left.append(
                lax.ppermute(
                    hold(left[-1]), "ctx", [(n - 1 - i, n - 2 - i) for i in range(k - 1, n - 1)]
                )
            )
            hold = yield (right[-1], left[-1])
        shape = list(own.shape)
        shape.insert(axis, n)
        out = jnp.zeros(shape, F32)
        for k in range(n):
            if k == 0:
                piece = own.astype(F32)
            else:
                piece = right[k].astype(F32) + left[n - k].astype(F32)
            out = lax.dynamic_update_slice_in_dim(
                out, jnp.expand_dims(piece, axis), (c_index - k) % n, axis
            )
        box.append(out)

    def butterfly_steps(value, combine, axes, box):
        hold = yield None
        for axis in axes:
            distance = 1
            while distance < sizes[axis]:
                got = flip(hold(value), axis, distance)
                value = combine(value, got)
                distance *= 2
                hold = yield (got,)
        box.append(value)

    def run_steps(jobs):
        live = []
        for first, job in jobs:
            next(job)
            live.append((first, job))
        step, marker = 1, None
        while live:
            seen, rest = [], []
            held = marker
            hold = (lambda x: after(x, held)) if held else (lambda x: x)
            for first, job in live:
                if first > step:
                    rest.append((first, job))
                    continue
                try:
                    seen.extend(job.send(hold))
                    rest.append((first, job))
                except StopIteration:
                    pass
            live, marker, step = rest, tuple(seen), step + 1

    def local(
        inputs,
        segments,
        norm_attn,
        query_weight,
        key_weight,
        value_weight,
        out_weight,
        norm_mlp,
        gate_weight,
        up_weight,
        down_weight,
        thresholds,
        cotangent,
    ):
        piece_len, seq_count, model_width = inputs.shape
        row_count = piece_len * seq_count
        f_index = lax.axis_index("fsdp")
        c_index = lax.axis_index("ctx")
        shard = model_width // fs
        q_cols = query_weight.shape[1]
        k_cols = key_weight.shape[1]
        heads_local = q_cols // HD
        groups_local = k_cols // HD
        group_size = heads_local // groups_local
        hidden_slice = gate_weight.shape[1] // fs
        full_len = piece_len * cs
        longest = full_len // 2
        back = min(cs - 1, (longest + piece_len - 2) // piece_len)
        shift_right = [(i, i + 1) for i in range(cs - 1)]
        shift_left = [(i + 1, i) for i in range(cs - 1)]

        qkv_parts = gather_near(jnp.concatenate([query_weight, key_weight, value_weight], axis=1))
        gains = place(
            gather_near(jnp.stack([norm_attn, norm_mlp])), f_index, 1
        ).astype(F32)
        gain_one = gains[0]
        gain_two = gains[1]
        qkv_full = place(qkv_parts, f_index, 0)
        positions = c_index * piece_len + jnp.arange(piece_len, dtype=jnp.int32)
        cosine, sine_table = rope_angles(positions, HD)
        flat_in = inputs.astype(F32).reshape(row_count, model_width)
        scale_one = rms_scale(flat_in)
        normed_one = flat_in * scale_one
        hidden_one = (normed_one * gain_one).astype(BF16)
        qkv_lin = matmul_plain(hidden_one, qkv_full)
        out_parts, _ = gather_shared(after(out_weight, qkv_parts[1]), c_index, qkv_lin)
        grad_top = cotangent.astype(F32).reshape(row_count, model_width)
        grad_mlp = after((RESIDUAL * grad_top).astype(BF16), qkv_lin)
        grad_mlp_all = jnp.concatenate(gather_near(grad_mlp), axis=0)
        value_vec = qkv_lin[:, q_cols + k_cols :].astype(BF16)
        queries = rotate(
            qkv_lin[:, :q_cols].reshape(piece_len, seq_count, heads_local, HD),
            cosine,
            sine_table,
            1.0,
        ).astype(BF16)
        key_rot = rotate(
            qkv_lin[:, q_cols : q_cols + k_cols].reshape(piece_len, seq_count, groups_local, HD),
            cosine,
            sine_table,
            1.0,
        ).astype(BF16)
        grouped_q = queries.reshape(piece_len, seq_count, groups_local, group_size, HD)
        kv_list = [
            jnp.stack(
                [key_rot, value_vec.reshape(piece_len, seq_count, groups_local, HD)]
            )
        ]
        seg_own = segments.T
        seg_list = [seg_own]
        for r in range(back):
            kv_list.append(lax.ppermute(kv_list[-1], "ctx", shift_right))
            seg_list.append(lax.ppermute(seg_list[-1], "ctx", shift_right))
        kv_all = jnp.concatenate(kv_list, axis=1)
        seg_all = jnp.concatenate(seg_list, axis=0)
        key_all, value_all = kv_all[0], kv_all[1]
        offsets = jnp.repeat(jnp.arange(back + 1, dtype=jnp.int32), piece_len)
        key_pos = jnp.tile(positions, back + 1) - offsets * piece_len
        allowed = (
            (seg_own[:, :, None] == seg_all.T[None, :, :])
            & (key_pos >= 0)[None, None, :]
            & ((positions // BLOCK)[:, None] >= (key_pos // BLOCK)[None, :])[:, None, :]
        )[:, :, None, None, :]
        scores = (
            jnp.einsum("cshgd,kshd->cshgk", grouped_q, key_all, preferred_element_type=F32)
            * ATTN_SCALE
        )
        masked = jnp.where(allowed, scores, NEG_FILL)
        run_peak = jnp.max(masked, axis=-1)
        weights_raw = jnp.exp(masked - run_peak[..., None])
        run_total = jnp.sum(weights_raw, axis=-1)
        out_f32 = (
            jnp.einsum(
                "cshgk,kshd->cshgd", weights_raw.astype(BF16), value_all, preferred_element_type=F32
            )
            / run_total[..., None]
        )
        log_total = run_peak + jnp.log(run_total)
        top_seen = jnp.max(run_peak, axis=(0, 1)).reshape(heads_local)
        out_full = place(out_parts, f_index, 1)
        attn_out = out_f32.reshape(row_count, heads_local * HD).astype(BF16)
        att_part = matmul_plain(attn_out, out_full).astype(BF16)
        gate_in, up_in = lax.optimization_barrier((gate_weight, up_weight, out_parts[1]))[:2]

        def gate_up_block(j, first, rows):
            start = (first, j * hidden_slice)
            return jnp.concatenate(
                [
                    lax.dynamic_slice(gate_in, start, (rows, hidden_slice)),
                    lax.dynamic_slice(up_in, start, (rows, hidden_slice)),
                ],
                axis=1,
            )

        gate_up_parts, _ = swap_shared(gate_up_block, shard, f_index, c_index, kv_list[-1], att_part)
        down_in = after(down_weight, qkv_lin)
        down_parts, _ = swap_shared(
            lambda j, first, rows: lax.dynamic_slice_in_dim(
                down_in, j * hidden_slice + first, rows, 0
            ),
            hidden_slice,
            f_index,
            c_index,
            out_f32,
            att_part,
        )

        gate_up_full = place(gate_up_parts, f_index, 0)
        down_full = place(down_parts, f_index, 1)
        attn_sum = tp_sum(att_part)
        middle = flat_in + RESIDUAL * attn_sum
        scale_two = rms_scale(middle)
        normed_two = middle * scale_two
        hidden_two = (normed_two * gain_two).astype(BF16)

        def own_wide(grad):
            parts = swap_near(
                lambda j: lax.dynamic_slice_in_dim(grad, j * shard, shard, 0), f_index
            )
            return place(parts, f_index, 1)

        hidden_all = jnp.concatenate(gather_near(hidden_two), axis=0)
        gate_up_val = matmul_plain(hidden_all, gate_up_full)
        gate_val = gate_up_val[:, :hidden_slice]
        up_val = gate_up_val[:, hidden_slice:]
        gate_sig = jax.nn.sigmoid(gate_val)
        activated = gate_val * gate_sig
        inner_act = (activated * up_val).astype(BF16)
        down_grad = contract_rows(inner_act, grad_mlp_all).astype(BF16)
        grad_inner = contract_cols(after(grad_mlp_all, down_grad), down_full)
        grad_gate = (grad_inner * up_val * gate_sig * (1.0 + gate_val * (1.0 - gate_sig))).astype(
            BF16
        )
        grad_upv = (grad_inner * activated).astype(BF16)
        grad_gate_up = jnp.concatenate([grad_gate, grad_upv], axis=1)
        back_part = contract_cols(grad_gate_up, gate_up_full).astype(BF16)
        back_part = back_part.reshape(fs, row_count, model_width)
        hidden_two_sum = reduce_near([back_part[d] for d in range(fs)])
        grad_hidden_two = tp_sum(hidden_two_sum)

        gate_grad = contract_rows(hidden_all, grad_gate).astype(BF16)
        up_grad = contract_rows(hidden_all, grad_upv).astype(BF16)
        marks = []

        mlp_part = matmul_plain(inner_act, down_full).astype(BF16)
        mlp_part = mlp_part.reshape(fs, row_count, model_width)
        mlp_sum = tp_sum(reduce_near([mlp_part[d] for d in range(fs)]))
        output = (
            (middle + RESIDUAL * mlp_sum).astype(BF16).reshape(piece_len, seq_count, model_width)
        )

        grad_gain_mlp = jnp.sum(grad_hidden_two * normed_two, axis=0)
        grad_middle = grad_top + norm_back(grad_hidden_two, normed_two, scale_two, gain_two)
        grad_attn = (RESIDUAL * grad_middle).astype(BF16)
        grad_heads = (
            contract_cols(grad_attn, out_full)
            .astype(BF16)
            .reshape(piece_len, seq_count, groups_local, group_size, HD)
        )
        out_grad = contract_rows(attn_out, grad_attn).astype(BF16)
        out_own = (
            reduce_near(
                [
                    lax.dynamic_slice_in_dim(out_grad, (f_index ^ d) * shard, shard, 1)
                    for d in range(fs)
                ]
            )
        )
        row_dot = jnp.sum(grad_heads.astype(F32) * out_f32, axis=-1)
        weights_now = jnp.exp(masked - log_total[..., None])
        grad_values = jnp.einsum(
            "cshgk,cshgd->kshd", weights_now.astype(BF16), grad_heads, preferred_element_type=F32
        )
        grad_weights = jnp.einsum(
            "cshgd,kshd->cshgk", grad_heads, value_all, preferred_element_type=F32
        )
        grad_scores = (weights_now * (grad_weights - row_dot[..., None])).astype(BF16)
        grad_query = (
            jnp.einsum("cshgk,kshd->cshgd", grad_scores, key_all, preferred_element_type=F32)
            * ATTN_SCALE
        )
        grad_keys = (
            jnp.einsum("cshgk,cshgd->kshd", grad_scores, grouped_q, preferred_element_type=F32)
            * ATTN_SCALE
        )
        kv_grad = jnp.stack([grad_keys, grad_values]).reshape(
            2, back + 1, piece_len, seq_count, groups_local, HD
        )
        carried = None
        for r in range(back, 0, -1):
            sent = kv_grad[:, r]
            if carried is not None:
                sent = sent + carried.astype(F32)
            carried = lax.ppermute(sent.astype(BF16), "ctx", shift_left)
        kv_own = kv_grad[:, 0]
        if carried is not None:
            kv_own = kv_own + carried.astype(F32)
        grad_query_lin = rotate(
            grad_query.reshape(piece_len, seq_count, heads_local, HD), cosine, sine_table, -1.0
        ).reshape(row_count, q_cols)
        grad_key_lin = rotate(kv_own[0], cosine, sine_table, -1.0).reshape(row_count, k_cols)
        grad_qkv_lin = jnp.concatenate(
            [
                grad_query_lin.astype(BF16),
                grad_key_lin.astype(BF16),
                kv_own[1].reshape(row_count, k_cols).astype(BF16),
            ],
            axis=1,
        )
        qkv_grad = contract_rows(hidden_one, grad_qkv_lin).astype(BF16)
        qkv_sum = (
            reduce_near(
                [
                    lax.dynamic_slice_in_dim(qkv_grad, (f_index ^ d) * shard, shard, 0)
                    for d in range(fs)
                ]
            )
        )
        grad_hidden_one = tp_sum(contract_cols(grad_qkv_lin, qkv_full))
        grad_gain_attn = jnp.sum(grad_hidden_one * normed_one, axis=0)
        input_grad = (
            grad_middle + norm_back(grad_hidden_one, normed_one, scale_one, gain_one)
        ).reshape(piece_len, seq_count, model_width)
        gain_fsdp = butterfly(jnp.stack([grad_gain_attn, grad_gain_mlp]), "fsdp", jnp.add)
        gain_fsdp = lax.dynamic_slice_in_dim(gain_fsdp, f_index * shard, shard, 1)

        def down_mid(low):
            parts = swap_near(
                lambda j: lax.dynamic_slice_in_dim(low, j * shard, shard, 1), f_index
            )
            marks.append(tuple(parts))
            return place([part[None] for part in parts], f_index, 0)

        def gate_mid(low):
            parts = swap_near(
                lambda j: lax.dynamic_index_in_dim(low, j, 0, keepdims=False), f_index
            )
            return place(parts, f_index, 1)

        boxes = [[] for _ in range(7)]
        if cs > 4:
            units = (down_grad, own_wide(gate_grad), own_wide(up_grad), out_own, qkv_sum)
            for box, unit in zip(boxes, units):
                part = lax.psum_scatter(
                    unit.astype(BF16), "ctx", scatter_dimension=0, tiled=True
                )
                axis = 0
                if unit is down_grad:
                    part, axis = down_mid(part), 1
                box.append(lax.all_gather(part, "ctx", axis=axis, tiled=False).astype(F32))
            boxes[5].append(butterfly(butterfly(top_seen, "fsdp", jnp.maximum), "ctx", jnp.maximum))
            boxes[6].append(butterfly(gain_fsdp, "ctx", jnp.add))
        else:
            jobs = [(1, line_total(down_grad, c_index, boxes[0], down_mid, 1))]
            starts = (1 + cs, 1 + 2 * cs, 2 + cs, 2 + 2 * cs)
            gate_chunks = gate_grad.reshape(fs, cs, shard // cs, hidden_slice)
            jobs.append((starts[0], line_total(gate_chunks, c_index, boxes[1], gate_mid)))
            units = (lambda: own_wide(after(up_grad, marks[0])), out_own, qkv_sum)
            for first, unit, box in zip(starts[1:], units, boxes[2:5]):
                jobs.append((first, line_total(unit, c_index, box)))
            jobs.append(
                (2 + 2 * cs, butterfly_steps(top_seen, jnp.maximum, ("fsdp", "ctx"), boxes[5]))
            )
            jobs.append((5 + 2 * cs, butterfly_steps(gain_fsdp, jnp.add, ("ctx",), boxes[6])))
            run_steps(jobs)
        (down_all,), (gate_all,), (up_all,), (out_all,), (qkv_all,) = boxes[:5]
        (head_peaks,), (gain_own,) = boxes[5:]
        grad_down_w = down_all.reshape(-1, shard)
        grad_gate_w = gate_all.reshape(shard, -1)
        grad_up_w = up_all.reshape(shard, -1)
        grad_out_w = out_all.reshape(-1, shard)
        qkv_own = qkv_all.reshape(shard, -1)

        ratio_clip = thresholds / jnp.maximum(head_peaks, thresholds)
        query_factor = jnp.repeat(jnp.sqrt(ratio_clip), HD)
        key_factor = jnp.repeat(
            jnp.sqrt(jnp.min(ratio_clip.reshape(groups_local, group_size), axis=1)), HD
        )
        clipped_query = (query_weight.astype(F32) * query_factor[None, :]).astype(BF16)
        clipped_key = (key_weight.astype(F32) * key_factor[None, :]).astype(BF16)
        return (
            output,
            input_grad,
            gain_own[0],
            qkv_own[:, :q_cols],
            qkv_own[:, q_cols : q_cols + k_cols],
            qkv_own[:, q_cols + k_cols :],
            grad_out_w,
            gain_own[1],
            grad_gate_w,
            grad_up_w,
            grad_down_w,
            head_peaks,
            clipped_query,
            clipped_key,
        )

    return local


def solution(mesh):
    placed = (
        P("ctx", "fsdp", None),
        P("fsdp", "ctx"),
        P("fsdp"),
        P("fsdp", "tp"),
        P("fsdp", "tp"),
        P("fsdp", "tp"),
        P("tp", "fsdp"),
        P("fsdp"),
        P("fsdp", "tp"),
        P("fsdp", "tp"),
        P("tp", "fsdp"),
        P("tp"),
        P("ctx", "fsdp", None),
    )
    return jax.shard_map(
        make_local({name: mesh.shape[name] for name in ("fsdp", "ctx", "tp")}),
        mesh=mesh,
        in_specs=placed,
        out_specs=(
            P("ctx", "fsdp", None),
            P("ctx", "fsdp", None),
            P("fsdp"),
            P("fsdp", "tp"),
            P("fsdp", "tp"),
            P("fsdp", "tp"),
            P("tp", "fsdp"),
            P("fsdp"),
            P("fsdp", "tp"),
            P("fsdp", "tp"),
            P("tp", "fsdp"),
            P("tp"),
            P("fsdp", "tp"),
            P("fsdp", "tp"),
        ),
        check_vma=False,
    )
```
